32 devices in a mesh: dp: 8 (over z, y), tensor: 4 (over x, core).
Axes of the slice: x: 2, y: 2, z: 4, core: 2. Of those that a mesh axis runs over, the one named last changes fastest.
Arguments:
- token_ids: int32 [256, 512], P('dp'), may hold values from 0 to 31999
- lengths: int32 [256], P('dp'), may hold values from 128 to 512
- table: bfloat16 [1024, 32000], P('tensor'), may hold values from -6 to 6
- cotangent: bfloat16 [256, 1024, 256], P('dp', 'tensor'), may hold values from -6 to 6
- proj_a: bfloat16 [1024, 64], P('tensor'), may hold values from -0.1875 to 0.1875
- proj_b: bfloat16 [1024, 5, 64], P('tensor'), may hold values from -0.078125 to 0.078125
Outputs:
- similarity: float32 [256, 256], P(('dp', 'tensor'))
The draws below stay inside these ranges and needn't reach their ends.
Inputs may be any that keep to these rules, and one draw needn't show every extreme that they name: `lengths`: each recipe has at least a quarter of its positions live.
All inputs are finite; a program needn't handle non-finite values.
Results may differ from the reference program's by a relative error of at most 0.0012.
Values may be sent and summed in bfloat16 or wider, within the bound.
A program may use at most 320 MiB of HBM per device.

```python
import math
import jax
import jax.numpy as jnp
import numpy as np
from jax import lax

CH = 1024
KERNEL = 5
PROJ = 64
VOCAB = 32000
SEQ = 512
T_OUT = 256
FEATS = 4096
RECIPES = 256


def touch_ends(drawn, stream_key, smallest, top_value):
    longest = drawn.shape.index(max(drawn.shape))
    spots = []
    for shift in (0, 1):
        where = [jax.random.randint(jax.random.fold_in(stream_key, axis), (), 0, length) for axis, length in enumerate(drawn.shape)]
        where[longest] = (where[longest] + shift) % drawn.shape[longest]
        spots.append(tuple(where))
    return drawn.at[spots[0]].set(smallest).at[spots[1]].set(top_value)


def block_levels(key, dims, shards, smallest, top_value):
    gain, own = 1.0, jax.random.fold_in(key, 6)
    for axis_at, blocks in shards:
        heights = jnp.exp(jax.random.uniform(jax.random.fold_in(own, axis_at), (blocks,), jnp.float32, smallest / len(shards), top_value / len(shards)))
        gain = gain * jnp.repeat(heights, dims[axis_at] // blocks).reshape([-1 if axis == axis_at else 1 for axis in range(len(dims))])
    return gain


def rank_bounds(amount, slope):
    portions = [(1 << 20) // math.isqrt(grade ** slope) + 1 for grade in range(1, amount + 1)]
    deviation = 1 + sum(portions) // (1 << 30)
    return np.cumsum(np.array([max(1, weight // deviation) for weight in portions]))


def ranked_ids(own_key, dims, number_of, slope):
    table = rank_bounds(number_of, slope)
    pick = jax.random.randint(jax.random.fold_in(own_key, 1), dims, 0, int(table[number_of - 1]))
    grade = jnp.searchsorted(jnp.asarray(table, jnp.int32), pick, side="right")
    return jax.random.permutation(jax.random.fold_in(own_key, 2), number_of)[grade].astype(jnp.int32)


def normal_values(own_key, extent, width, limit, split=(), kind=jnp.bfloat16):
    loudness = block_levels(own_key, extent, split, -0.22, 0.18) if split else 1.0
    drawn = jax.random.normal(own_key, extent, jnp.float32) * width * loudness
    return jnp.minimum(jnp.maximum(drawn, -limit), limit).astype(kind)


def setup_inputs(seed: int = 0) -> dict:
    arg_keys = jax.random.split(jax.random.key(seed), 7)
    token_ids = touch_ends(ranked_ids(arg_keys[0], (RECIPES, SEQ), VOCAB, 2), jax.random.fold_in(arg_keys[0], 3), 0, VOCAB - 1).astype(jnp.int32)
    lengths = touch_ends(jax.random.randint(arg_keys[1], (RECIPES,), SEQ // 4, SEQ + 1), jax.random.fold_in(arg_keys[1], 1), SEQ // 4, SEQ).astype(jnp.int32)
    table = normal_values(arg_keys[2], (CH, VOCAB), 1.0, 6.0, ((0, 4),))
    cotangent = normal_values(arg_keys[3], (RECIPES, CH, T_OUT), 1.0, 6.0, ((0, 8), (1, 4)))
    proj_a = normal_values(arg_keys[4], (CH, PROJ), CH ** -0.5, 0.1875, ((0, 4),))
    proj_b = normal_values(arg_keys[5], (CH, KERNEL, PROJ), (CH * KERNEL) ** -0.5, 0.078125, ((0, 4),))
    return dict(token_ids=token_ids, lengths=lengths, table=table, cotangent=cotangent, proj_a=proj_a, proj_b=proj_b)


def block_features(ids_b, len_b, delta_b, table, proj_a, proj_b):
    count = ids_b.shape[0]
    pos = jnp.arange(SEQ, dtype=jnp.int32)
    keep = (pos[None, :] < len_b[:, None]).astype(table.dtype)
    embedded = jnp.take(table, ids_b, axis=1) * keep[None, :, :]
    padded = jnp.pad(embedded, ((0, 0), (0, 0), (KERNEL // 2, KERNEL // 2)))
    right = jnp.zeros((count, PROJ, T_OUT), jnp.float32)
    for k in range(KERNEL):
        tap = padded[:, :, k:k + SEQ:2]
        right = right + jnp.einsum('cnt,cb->nbt', tap.astype(jnp.float32), proj_b[:, k, :].astype(jnp.float32))
    outpos = 2 * jnp.arange(T_OUT, dtype=jnp.int32)
    tkeep = (outpos[None, :] < len_b[:, None]).astype(delta_b.dtype)
    masked = delta_b * tkeep[:, None, :]
    left = jnp.einsum('nct,ca->nat', masked.astype(jnp.float32), proj_a.astype(jnp.float32))
    raw = jnp.einsum('nat,nbt->nab', left, right, precision=lax.Precision.HIGHEST).reshape(count, FEATS)
    scale = lax.rsqrt(lax.optimization_barrier(jnp.mean(raw * raw, axis=1)) + 1e-06)
    return (raw * scale[:, None]).astype(jnp.bfloat16)

def reference(token_ids, lengths, table, cotangent, proj_a, proj_b):
    blocks = min(32, RECIPES)
    nblk = RECIPES // blocks
    ids_r = token_ids.reshape(nblk, blocks, SEQ)
    len_r = lengths.reshape(nblk, blocks)
    del_r = cotangent.reshape(nblk, blocks, CH, T_OUT)

    def one(parts):
        return block_features(parts[0], parts[1], parts[2], table, proj_a, proj_b)
    unit = lax.map(one, (ids_r, len_r, del_r)).reshape(RECIPES, FEATS)
    return jnp.dot(unit, unit.T, preferred_element_type=jnp.float32) * (1.0 / FEATS)
```

```python
import functools

import jax
import jax.numpy as jnp
from jax import lax
from jax.experimental import pallas as pl
from jax.experimental.pallas import tpu as pltpu
from jax.sharding import PartitionSpec as P

LANES = 128
UNROLL = 8
PAD = 8


def right_kernel(vocab, vblocks, group, steps_out, ids_ref, live_ref, table_ref, w_ref, out_ref, rows, near, far):
    step = pl.program_id(0)
    vblk = table_ref.shape[1]

    @pl.when(step < vblocks)
    def _():
        base = pl.multiple_of(step * vblk, LANES)
        part = lax.dot_general(
            table_ref[...], w_ref[...], (((0,), (0,)), ((), ())), preferred_element_type=jnp.float32
        )
        for col in range(3):
            rows[col, pl.ds(base, vblk), :] = part[:, col * LANES:(col + 1) * LANES]

    @pl.when(step == vblocks)
    def _():
        for col in range(3):
            rows[col, pl.ds(vocab, PAD), :] = jnp.zeros((PAD, LANES), jnp.float32)
        for side in range(2):
            near[side, pl.ds(0, PAD), :] = jnp.zeros((PAD, LANES), jnp.float32)
            far[side, pl.ds(PAD + steps_out, PAD), :] = jnp.zeros((PAD, LANES), jnp.float32)

    @pl.when(step >= vblocks)
    def _():
        lane = lax.broadcasted_iota(jnp.int32, (steps_out, LANES), 1)
        for pair in range(group // 2):
            for side in range(2):
                rec = (step - vblocks) * group + pair * 2 + side
                live = live_ref[rec]
                tiles = (live + (UNROLL - 1)) // UNROLL

                def clear(i, _):
                    at = pl.ds(pl.multiple_of(PAD + i * UNROLL, UNROLL), UNROLL)
                    near[side, at, :] = jnp.zeros((UNROLL, LANES), jnp.float32)
                    far[side, at, :] = jnp.zeros((UNROLL, LANES), jnp.float32)
                    return 0

                lax.fori_loop(tiles, steps_out // UNROLL, clear, 0)

                def fetch(i, _):
                    start = rec * (2 * steps_out) + i * (2 * UNROLL)
                    for u in range(UNROLL):
                        even = ids_ref[start + 2 * u]
                        odd = ids_ref[start + 2 * u + 1]
                        at = pl.ds(PAD + i * UNROLL + u, 1)
                        near[side, at, :] = rows[0, pl.ds(even, 1), :] + rows[1, pl.ds(odd, 1), :]
                        far[side, at, :] = rows[2, pl.ds(even, 1), :]
                    return 0

                lax.fori_loop(0, tiles, fetch, 0)
            own0 = near[0, pl.ds(PAD, steps_out), :]
            own1 = near[1, pl.ds(PAD, steps_out), :]
            edge0 = near[0, pl.ds(PAD - 1, steps_out), :] + far[0, pl.ds(PAD + 1, steps_out), :]
            edge1 = near[1, pl.ds(PAD - 1, steps_out), :] + far[1, pl.ds(PAD + 1, steps_out), :]
            first = own0 + pltpu.roll(edge0, LANES // 2, 1)
            second = pltpu.roll(own1, LANES // 2, 1) + edge1
            out_ref[pair] = jnp.where(lane < LANES // 2, first, second)


def right_pairs(ids, live, table, weights, steps_out):
    vocab = table.shape[1]
    chans = table.shape[0]
    recipes = live.shape[0]
    vblk = 1280
    vblocks = vocab // vblk
    group = 4
    return pl.pallas_call(
        functools.partial(right_kernel, vocab, vblocks, group, steps_out),
        grid_spec=pltpu.PrefetchScalarGridSpec(
            num_scalar_prefetch=2,
            grid=(vblocks + recipes // group,),
            in_specs=[
                pl.BlockSpec((chans, vblk), lambda s, *_: (0, jnp.minimum(s, vblocks - 1))),
                pl.BlockSpec((chans, 3 * LANES), lambda s, *_: (0, 0)),
            ],
            out_specs=pl.BlockSpec(
                (group // 2, steps_out, LANES), lambda s, *_: (jnp.maximum(s - vblocks, 0), 0, 0)
            ),
            scratch_shapes=[
                pltpu.VMEM((3, vocab + PAD, LANES), jnp.float32),
                pltpu.VMEM((2, steps_out + 2 * PAD, LANES), jnp.float32),
                pltpu.VMEM((2, steps_out + 2 * PAD, LANES), jnp.float32),
            ],
        ),
        out_shape=jax.ShapeDtypeStruct((recipes // 2, steps_out, LANES), jnp.float32),
        compiler_params=pltpu.CompilerParams(vmem_limit_bytes=60 * 1024 * 1024),
        cost_estimate=pl.CostEstimate(
            flops=2 * vocab * chans * 3 * LANES, bytes_accessed=200 * 1024 * 1024, transcendentals=0
        ),
    )(ids, live, table, weights)


def left_part_of(lengths, cotangent, proj_a):
    steps_out = cotangent.shape[2]
    outpos = 2 * jnp.arange(steps_out, dtype=jnp.int32)
    tkeep = outpos[None, :] < lengths[:, None]
    masked = jnp.where(tkeep[:, None, :], cotangent, jnp.zeros((), cotangent.dtype))
    return jnp.einsum("nct,ca->nat", masked, proj_a, preferred_element_type=jnp.float32)


def local(token_ids, lengths, table, cotangent, proj_a, proj_b):
    recipes_here, seqlen = token_ids.shape
    chans, width = proj_a.shape
    vocab = table.shape[1]
    steps_out = seqlen // 2
    total_feats = width * width
    left_part = left_part_of(lengths, cotangent, proj_a)
    left_own = lax.psum_scatter(left_part, "tensor", scatter_dimension=0, tiled=True)

    pos = jnp.arange(seqlen, dtype=jnp.int32)
    ids = jnp.where(pos[None, :] < lengths[:, None], token_ids, vocab).reshape(-1)
    live = (lengths + 1) // 2
    tap = [proj_b[:, k, :] for k in range(5)]
    weights = jnp.concatenate([tap[2], tap[0], tap[3], tap[1], jnp.zeros_like(tap[4]), tap[4]], axis=1)
    right_part = right_pairs(ids, live, table, weights, steps_out)
    right_own = lax.psum_scatter(right_part, "tensor", scatter_dimension=0, tiled=True)
    mine = right_own.shape[0] * 2
    left_two = left_own.reshape(mine // 2, 2, width, steps_out)
    raw = jnp.stack(
        [
            jnp.einsum(
                "nat,ntb->nab", left_two[:, side], right_own[:, :, side * width:(side + 1) * width],
                precision=lax.Precision.HIGHEST,
            )
            for side in range(2)
        ],
        axis=1,
    ).reshape(mine, total_feats)
    scale = lax.rsqrt(jnp.mean(raw * raw, axis=1) + 1e-06)
    unit = (raw * scale[:, None]).astype(jnp.bfloat16)
    every = lax.all_gather(unit, ("dp", "tensor"), axis=0, tiled=True)
    terms = lax.dot_general(
        unit, every, (((1,), (1,)), ((), ())), preferred_element_type=jnp.float32
    )
    return terms * (1.0 / total_feats)


def solution(mesh):
    placed = (
        P("dp", None),
        P("dp"),
        P("tensor", None),
        P("dp", "tensor", None),
        P("tensor", None),
        P("tensor", None, None),
    )
    return jax.shard_map(
        local, mesh=mesh, in_specs=placed, out_specs=P(("dp", "tensor"), None), check_vma=False
    )
```

```python
import functools

import jax
import jax.numpy as jnp
from jax import lax
from jax.experimental import pallas as pl
from jax.experimental.pallas import tpu as pltpu
from jax.sharding import PartitionSpec as P

LANES = 128
UNROLL = 8
PAD = 8


def right_kernel(vocab, vblocks, group, steps_out, ids_ref, live_ref, table_ref, w_ref, out_ref, rows, near, far):
    step = pl.program_id(0)
    vblk = table_ref.shape[1]

    @pl.when(step < vblocks)
    def _():
        base = pl.multiple_of(step * vblk, LANES)
        part = lax.dot_general(
            table_ref[...], w_ref[...], (((0,), (0,)), ((), ())), preferred_element_type=jnp.float32
        )
        for col in range(3):
            rows[col, pl.ds(base, vblk), :] = part[:, col * LANES:(col + 1) * LANES]

    @pl.when(step == vblocks)
    def _():
        for col in range(3):
            rows[col, pl.ds(vocab, PAD), :] = jnp.zeros((PAD, LANES), jnp.float32)
        for side in range(2):
            near[side, pl.ds(0, PAD), :] = jnp.zeros((PAD, LANES), jnp.float32)
            far[side, pl.ds(PAD + steps_out, PAD), :] = jnp.zeros((PAD, LANES), jnp.float32)

    @pl.when(step >= vblocks)
    def _():
        lane = lax.broadcasted_iota(jnp.int32, (steps_out, LANES), 1)
        for pair in range(group // 2):
            for side in range(2):
                rec = (step - vblocks) * group + pair * 2 + side
                live = live_ref[rec]
                tiles = (live + (UNROLL - 1)) // UNROLL

                def clear(i, _):
                    at = pl.ds(pl.multiple_of(PAD + i * UNROLL, UNROLL), UNROLL)
                    near[side, at, :] = jnp.zeros((UNROLL, LANES), jnp.float32)
                    far[side, at, :] = jnp.zeros((UNROLL, LANES), jnp.float32)
                    return 0

                lax.fori_loop(tiles, steps_out // UNROLL, clear, 0)

                def fetch(i, _):
                    start = rec * (2 * steps_out) + i * (2 * UNROLL)
                    for u in range(UNROLL):
                        even = ids_ref[start + 2 * u]
                        odd = ids_ref[start + 2 * u + 1]
                        at = pl.ds(PAD + i * UNROLL + u, 1)
                        near[side, at, :] = rows[0, pl.ds(even, 1), :] + rows[1, pl.ds(odd, 1), :]
                        far[side, at, :] = rows[2, pl.ds(even, 1), :]
                    return 0

                lax.fori_loop(0, tiles, fetch, 0)
            own0 = near[0, pl.ds(PAD, steps_out), :]
            own1 = near[1, pl.ds(PAD, steps_out), :]
            edge0 = near[0, pl.ds(PAD - 1, steps_out), :] + far[0, pl.ds(PAD + 1, steps_out), :]
            edge1 = near[1, pl.ds(PAD - 1, steps_out), :] + far[1, pl.ds(PAD + 1, steps_out), :]
            first = own0 + pltpu.roll(edge0, LANES // 2, 1)
            second = pltpu.roll(own1, LANES // 2, 1) + edge1
            out_ref[pair] = jnp.where(lane < LANES // 2, first, second)


def right_pairs(ids, live, table, weights, steps_out):
    vocab = table.shape[1]
    chans = table.shape[0]
    recipes = live.shape[0]
    vblk = 1280
    vblocks = vocab // vblk
    group = 4
    return pl.pallas_call(
        functools.partial(right_kernel, vocab, vblocks, group, steps_out),
        grid_spec=pltpu.PrefetchScalarGridSpec(
            num_scalar_prefetch=2,
            grid=(vblocks + recipes // group,),
            in_specs=[
                pl.BlockSpec((chans, vblk), lambda s, *_: (0, jnp.minimum(s, vblocks - 1))),
                pl.BlockSpec((chans, 3 * LANES), lambda s, *_: (0, 0)),
            ],
            out_specs=pl.BlockSpec(
                (group // 2, steps_out, LANES), lambda s, *_: (jnp.maximum(s - vblocks, 0), 0, 0)
            ),
            scratch_shapes=[
                pltpu.VMEM((3, vocab + PAD, LANES), jnp.float32),
                pltpu.VMEM((2, steps_out + 2 * PAD, LANES), jnp.float32),
                pltpu.VMEM((2, steps_out + 2 * PAD, LANES), jnp.float32),
            ],
        ),
        out_shape=jax.ShapeDtypeStruct((recipes // 2, steps_out, LANES), jnp.float32),
        compiler_params=pltpu.CompilerParams(vmem_limit_bytes=60 * 1024 * 1024),
        cost_estimate=pl.CostEstimate(
            flops=2 * vocab * chans * 3 * LANES, bytes_accessed=200 * 1024 * 1024, transcendentals=0
        ),
    )(ids, live, table, weights)


def share_kernel(dp_count, left_ref, part_ref, out_ref, core_in, core_own, cross_out, cross_in,
                 planes, packed, every, sums, got, core_send, core_recv, cross_send, cross_recv,
                 slice_send, slice_recv, wide_send, wide_recv, row_send, row_recv):
    me = lax.axis_index("tensor")
    block = lax.axis_index("dp")
    sib = me + 1 - 2 * (me % 2)
    across = (me + 2) % 4
    diag = (sib + 2) % 4
    pairs = left_ref.shape[0]
    half = LANES // 2
    feats = half * half
    mesh_ids = pl.DeviceIdType.MESH

    barrier = pltpu.get_barrier_semaphore()
    for off in range(1, 4):
        pl.semaphore_signal(barrier, inc=1, device_id={"tensor": (me + off) % 4}, device_id_type=mesh_ids)
    for off in range(1, dp_count):
        pl.semaphore_signal(barrier, inc=1, device_id={"dp": (block + off) % dp_count}, device_id_type=mesh_ids)
    pl.semaphore_wait(barrier, 3 + dp_count - 1)

    def remote(src, dst, send, recv, where):
        return pltpu.make_async_remote_copy(
            src_ref=src, dst_ref=dst, send_sem=send, recv_sem=recv, device_id=where, device_id_type=mesh_ids
        )

    first = [
        remote(part_ref.at[diag * pairs + i], core_in.at[i], core_send.at[i], core_recv.at[i], {"tensor": sib})
        for i in range(pairs)
    ]
    second = [
        remote(part_ref.at[sib * pairs + i], core_own.at[i], core_send.at[pairs + i], core_recv.at[pairs + i],
               {"tensor": sib})
        for i in range(pairs)
    ]
    for copy in first + second:
        copy.start()
    over = [
        remote(cross_out.at[i], cross_in.at[i], cross_send.at[i], cross_recv.at[i], {"tensor": across})
        for i in range(pairs)
    ]
    for i in range(pairs):
        first[i].wait_recv()
        cross_out[i] = (part_ref[across * pairs + i] + core_in[i]).astype(jnp.bfloat16)
        over[i].start()

    lane = lax.broadcasted_iota(jnp.int32, (half // 2, LANES), 1) < half
    quarter = half // 2
    for i in range(pairs):
        second[i].wait_recv()
        mine = part_ref[me * pairs + i] + core_own[i]
        over[i].wait_recv()
        right = mine + cross_in[i].astype(jnp.float32)
        raw = lax.dot_general(
            left_ref[i], right, (((1,), (0,)), ((), ())),
            precision=lax.Precision.HIGHEST, preferred_element_type=jnp.float32,
        )
        top = jnp.where(lane, raw[:quarter], pltpu.roll(raw[quarter:half], half, 1))
        low = jnp.where(lane, pltpu.roll(raw[half:half + quarter], half, 1), raw[half + quarter:])
        for side, vals in enumerate((top, low)):
            total = jnp.sum(jnp.sum(vals * vals, axis=0, keepdims=True), axis=1, keepdims=True)
            planes[:, 2 * i + side, :] = vals * lax.rsqrt(total / feats + 1e-06)

    depth = packed.shape[1]
    for j in range(4):
        packed[j] = planes[j * depth:(j + 1) * depth].astype(jnp.bfloat16)
    every[block, me] = packed[me]
    slices = []
    for off in range(1, 4):
        peer = (me + off) % 4
        slices.append(
            remote(packed.at[peer], every.at[block, me], slice_send.at[off - 1], slice_recv.at[off - 1],
                   {"tensor": peer})
        )
    for copy in slices:
        copy.start()
    for copy in slices:
        copy.wait_recv()
    wide = [
        remote(every.at[block], every.at[block], wide_send.at[off - 1], wide_recv.at[off - 1],
               {"dp": (block + off) % dp_count})
        for off in range(1, dp_count)
    ]
    for copy in wide:
        copy.start()
    for copy in wide:
        copy.wait_recv()

    recs = packed.shape[2]
    total = jnp.zeros((4 * recs, dp_count * 4 * recs), jnp.float32)
    for plane in range(depth):
        lhs = every[block, :, plane].astype(jnp.float32).reshape(4 * recs, LANES).astype(jnp.bfloat16)
        rhs = every[:, :, plane].astype(jnp.float32).reshape(dp_count * 4 * recs, LANES).astype(jnp.bfloat16)
        total += lax.dot_general(lhs, rhs, (((1,), (1,)), ((), ())), preferred_element_type=jnp.float32)
    for j in range(4):
        sums[j] = total[j * recs:(j + 1) * recs]
    rows = []
    for off in range(1, 4):
        peer = (me + off) % 4
        rows.append(
            remote(sums.at[peer], got.at[off - 1], row_send.at[off - 1], row_recv.at[off - 1], {"tensor": peer})
        )
    for copy in rows:
        copy.start()
    result = sums[me]
    for off in range(3):
        rows[off].wait_recv()
        result = result + got[off]
    out_ref[...] = result
    for copy in first + second + over + slices + wide + rows:
        copy.wait_send()


def share(left_two, right_part, dp_count):
    pairs, _, steps_out = left_two.shape
    recs = 2 * pairs
    depth = LANES // 16
    vmem = pl.BlockSpec(memory_space=pltpu.VMEM)
    dma = pltpu.SemaphoreType.DMA
    return pl.pallas_call(
        functools.partial(share_kernel, dp_count),
        out_shape=jax.ShapeDtypeStruct((recs, dp_count * 4 * recs), jnp.float32),
        in_specs=[vmem, vmem],
        out_specs=vmem,
        scratch_shapes=[
            pltpu.VMEM((pairs, steps_out, LANES), jnp.float32),
            pltpu.VMEM((pairs, steps_out, LANES), jnp.float32),
            pltpu.VMEM((pairs, steps_out, LANES), jnp.bfloat16),
            pltpu.VMEM((pairs, steps_out, LANES), jnp.bfloat16),
            pltpu.VMEM((4 * depth, recs, LANES), jnp.float32),
            pltpu.VMEM((4, depth, recs, LANES), jnp.bfloat16),
            pltpu.VMEM((dp_count, 4, depth, recs, LANES), jnp.bfloat16),
            pltpu.VMEM((4, recs, dp_count * 4 * recs), jnp.float32),
            pltpu.VMEM((3, recs, dp_count * 4 * recs), jnp.float32),
            dma((2 * pairs,)), dma((2 * pairs,)), dma((pairs,)), dma((pairs,)),
            dma((3,)), dma((3,)), dma((dp_count - 1,)), dma((dp_count - 1,)), dma((3,)), dma((3,)),
        ],
        compiler_params=pltpu.CompilerParams(
            collective_id=0, has_side_effects=True, vmem_limit_bytes=40 * 1024 * 1024
        ),
    )(left_two, right_part)


def left_part_of(lengths, cotangent, proj_a):
    steps_out = cotangent.shape[2]
    outpos = 2 * jnp.arange(steps_out, dtype=jnp.int32)
    tkeep = outpos[None, :] < lengths[:, None]
    masked = jnp.where(tkeep[:, None, :], cotangent, jnp.zeros((), cotangent.dtype))
    return jnp.einsum("nct,ca->nat", masked, proj_a, preferred_element_type=jnp.float32)


def local(token_ids, lengths, table, cotangent, proj_a, proj_b):
    recipes_here, seqlen = token_ids.shape
    chans, width = proj_a.shape
    vocab = table.shape[1]
    steps_out = seqlen // 2
    total_feats = width * width
    left_part = left_part_of(lengths, cotangent, proj_a)

    pos = jnp.arange(seqlen, dtype=jnp.int32)
    ids = jnp.where(pos[None, :] < lengths[:, None], token_ids, vocab).reshape(-1)
    live = (lengths + 1) // 2
    tap = [proj_b[:, k, :] for k in range(5)]
    weights = jnp.concatenate([tap[2], tap[0], tap[3], tap[1], jnp.zeros_like(tap[4]), tap[4]], axis=1)
    weights, left_part = lax.optimization_barrier((weights, left_part))
    left_own = lax.psum_scatter(left_part, "tensor", scatter_dimension=0, tiled=True)
    right_part = right_pairs(ids, live, table, weights, steps_out)
    if lax.axis_size("tensor") == 4:
        mine = left_own.shape[0]
        paired = left_own.reshape(mine // 2, 2 * width, steps_out)
        return share(paired, right_part, lax.axis_size("dp")) * (1.0 / total_feats)
    right_own = lax.psum_scatter(right_part, "tensor", scatter_dimension=0, tiled=True)
    mine = right_own.shape[0] * 2
    left_two = left_own.reshape(mine // 2, 2, width, steps_out)
    raw = jnp.stack(
        [
            jnp.einsum(
                "nat,ntb->nab", left_two[:, side], right_own[:, :, side * width:(side + 1) * width],
                precision=lax.Precision.HIGHEST,
            )
            for side in range(2)
        ],
        axis=1,
    ).reshape(mine, total_feats)
    scale = lax.rsqrt(jnp.mean(raw * raw, axis=1) + 1e-06)
    unit = (raw * scale[:, None]).astype(jnp.bfloat16)
    every = lax.all_gather(unit, ("dp", "tensor"), axis=0, tiled=True)
    terms = lax.dot_general(
        unit, every, (((1,), (1,)), ((), ())), preferred_element_type=jnp.float32
    )
    return terms * (1.0 / total_feats)


def solution(mesh):
    placed = (
        P("dp", None),
        P("dp"),
        P("tensor", None),
        P("dp", "tensor", None),
        P("tensor", None),
        P("tensor", None, None),
    )
    return jax.shard_map(
        local, mesh=mesh, in_specs=placed, out_specs=P(("dp", "tensor"), None), check_vma=False
    )
```

```python
import functools

import jax
import jax.numpy as jnp
from jax import lax
from jax.experimental import pallas as pl
from jax.experimental.pallas import tpu as pltpu
from jax.sharding import PartitionSpec as P

LANES = 128
UNROLL = 8
PAD = 8
CHUNK = 640


def right_kernel(vocab, vblocks, group, steps_out, ids_ref, live_ref, table_ref, w_ref, out_ref, rows, near, far, wts):
    step = pl.program_id(0)
    vblk = table_ref.shape[1]

    @pl.when(step == 0)
    def _():
        tap = [w_ref[k] for k in range(5)]
        wts[...] = jnp.concatenate([tap[2], tap[0], tap[3], tap[1], jnp.zeros_like(tap[4]), tap[4]], axis=0)

    @pl.when(step < vblocks)
    def _():
        def project(i, _):
            at = pl.multiple_of(i * CHUNK, LANES)
            base = pl.multiple_of(step * vblk + at, LANES)
            part = lax.dot_general(
                table_ref[:, pl.ds(at, CHUNK)], wts[...], (((0,), (1,)), ((), ())),
                preferred_element_type=jnp.float32,
            )
            for col in range(3):
                rows[col, pl.ds(base, CHUNK), :] = part[:, col * LANES:(col + 1) * LANES]
            return 0

        lax.fori_loop(0, vblk // CHUNK, project, 0, unroll=True)

    @pl.when(step == vblocks)
    def _():
        for col in range(3):
            rows[col, pl.ds(vocab, PAD), :] = jnp.zeros((PAD, LANES), jnp.float32)
        for side in range(2):
            near[side, pl.ds(0, PAD), :] = jnp.zeros((PAD, LANES), jnp.float32)
            far[side, pl.ds(PAD + steps_out, PAD), :] = jnp.zeros((PAD, LANES), jnp.float32)

    @pl.when(step >= vblocks)
    def _():
        lane = lax.broadcasted_iota(jnp.int32, (steps_out, LANES), 1)
        for pair in range(group // 2):
            for side in range(2):
                rec = (step - vblocks) * group + pair * 2 + side
                live = live_ref[rec]
                tiles = (live + (UNROLL - 1)) // UNROLL

                def clear(i, _):
                    at = pl.ds(pl.multiple_of(PAD + i * UNROLL, UNROLL), UNROLL)
                    near[side, at, :] = jnp.zeros((UNROLL, LANES), jnp.float32)
                    far[side, at, :] = jnp.zeros((UNROLL, LANES), jnp.float32)
                    return 0

                lax.fori_loop(tiles, steps_out // UNROLL, clear, 0)

                def fetch(i, _):
                    start = i * (2 * UNROLL)
                    for u in range(UNROLL):
                        even = ids_ref[rec, start + 2 * u]
                        odd = ids_ref[rec, start + 2 * u + 1]
                        at = pl.ds(PAD + i * UNROLL + u, 1)
                        near[side, at, :] = rows[0, pl.ds(even, 1), :] + rows[1, pl.ds(odd, 1), :]
                        far[side, at, :] = rows[2, pl.ds(even, 1), :]
                    return 0

                lax.fori_loop(0, tiles, fetch, 0)
            own0 = near[0, pl.ds(PAD, steps_out), :]
            own1 = near[1, pl.ds(PAD, steps_out), :]
            edge0 = near[0, pl.ds(PAD - 1, steps_out), :] + far[0, pl.ds(PAD + 1, steps_out), :]
            edge1 = near[1, pl.ds(PAD - 1, steps_out), :] + far[1, pl.ds(PAD + 1, steps_out), :]
            first = own0 + pltpu.roll(edge0, LANES // 2, 1)
            second = pltpu.roll(own1, LANES // 2, 1) + edge1
            out_ref[pair] = jnp.where(lane < LANES // 2, first, second)


def right_pairs(ids, live, table, weights, steps_out):
    vocab = table.shape[1]
    chans = table.shape[0]
    recipes = live.shape[0]
    vblk = 5 * CHUNK
    vblocks = vocab // vblk
    group = 4
    return pl.pallas_call(
        functools.partial(right_kernel, vocab, vblocks, group, steps_out),
        grid_spec=pltpu.PrefetchScalarGridSpec(
            num_scalar_prefetch=2,
            grid=(vblocks + recipes // group,),
            in_specs=[
                pl.BlockSpec((chans, vblk), lambda s, *_: (0, jnp.minimum(s, vblocks - 1))),
                pl.BlockSpec(weights.shape, lambda s, *_: (0, 0, 0)),
            ],
            out_specs=pl.BlockSpec(
                (group // 2, steps_out, LANES), lambda s, *_: (jnp.maximum(s - vblocks, 0), 0, 0)
            ),
            scratch_shapes=[
                pltpu.VMEM((3, vocab + PAD, LANES), jnp.float32),
                pltpu.VMEM((2, steps_out + 2 * PAD, LANES), jnp.float32),
                pltpu.VMEM((2, steps_out + 2 * PAD, LANES), jnp.float32),
                pltpu.VMEM((3 * LANES, chans), jnp.bfloat16),
            ],
        ),
        out_shape=jax.ShapeDtypeStruct((recipes // 2, steps_out, LANES), jnp.float32),
        compiler_params=pltpu.CompilerParams(vmem_limit_bytes=60 * 1024 * 1024),
        cost_estimate=pl.CostEstimate(
            flops=2 * vocab * chans * 3 * LANES, bytes_accessed=200 * 1024 * 1024, transcendentals=0
        ),
    )(ids, live, table, weights)


def share_kernel(dp_count, left_ref, left_b, left_c, left_d, part_ref, out_ref, core_in, core_own, cross_out, cross_in,
                 planes, packed, every, sums, got, core_send, core_recv, cross_send, cross_recv,
                 slice_send, slice_recv, wide_send, wide_recv, row_send, row_recv):
    me = lax.axis_index("tensor")
    block = lax.axis_index("dp")
    sib = me + 1 - 2 * (me % 2)
    across = (me + 2) % 4
    diag = (sib + 2) % 4
    pairs = left_ref.shape[0]
    half = LANES // 2
    feats = half * half
    mesh_ids = pl.DeviceIdType.MESH

    barrier = pltpu.get_barrier_semaphore()
    for off in range(1, 4):
        pl.semaphore_signal(barrier, inc=1, device_id={"tensor": (me + off) % 4}, device_id_type=mesh_ids)
    for off in range(1, dp_count):
        pl.semaphore_signal(barrier, inc=1, device_id={"dp": (block + off) % dp_count}, device_id_type=mesh_ids)
    pl.semaphore_wait(barrier, 3 + dp_count - 1)

    def remote(src, dst, send, recv, where):
        return pltpu.make_async_remote_copy(
            src_ref=src, dst_ref=dst, send_sem=send, recv_sem=recv, device_id=where, device_id_type=mesh_ids
        )

    first = [
        remote(part_ref.at[diag * pairs + i], core_in.at[i], core_send.at[i], core_recv.at[i], {"tensor": sib})
        for i in range(pairs)
    ]
    second = [
        remote(part_ref.at[sib * pairs + i], core_own.at[i], core_send.at[pairs + i], core_recv.at[pairs + i],
               {"tensor": sib})
        for i in range(pairs)
    ]
    for copy in first + second:
        copy.start()
    over = [
        remote(cross_out.at[i], cross_in.at[i], cross_send.at[i], cross_recv.at[i], {"tensor": across})
        for i in range(pairs)
    ]
    for i in range(pairs):
        first[i].wait_recv()
        cross_out[i] = (part_ref[across * pairs + i] + core_in[i]).astype(jnp.bfloat16)
        over[i].start()

    lane = lax.broadcasted_iota(jnp.int32, (half // 2, LANES), 1) < half
    quarter = half // 2
    for i in range(pairs):
        second[i].wait_recv()
        mine = part_ref[me * pairs + i] + core_own[i]
        over[i].wait_recv()
        right = mine + cross_in[i].astype(jnp.float32)
        raw = lax.dot_general(
            (left_ref[i] + left_b[i]) + (left_c[i] + left_d[i]), right, (((1,), (0,)), ((), ())),
            precision=lax.Precision.HIGHEST, preferred_element_type=jnp.float32,
        )
        top = jnp.where(lane, raw[:quarter], pltpu.roll(raw[quarter:half], half, 1))
        low = jnp.where(lane, pltpu.roll(raw[half:half + quarter], half, 1), raw[half + quarter:])
        for side, vals in enumerate((top, low)):
            total = jnp.sum(jnp.sum(vals * vals, axis=0, keepdims=True), axis=1, keepdims=True)
            planes[:, 2 * i + side, :] = vals * lax.rsqrt(total / feats + 1e-06)

    depth = packed.shape[1]
    for j in range(4):
        packed[j] = planes[j * depth:(j + 1) * depth].astype(jnp.bfloat16)
    every[block, me] = packed[me]
    slices = []
    for off in range(1, 4):
        peer = (me + off) % 4
        slices.append(
            remote(packed.at[peer], every.at[block, me], slice_send.at[off - 1], slice_recv.at[off - 1],
                   {"tensor": peer})
        )
    for copy in slices:
        copy.start()
    for copy in slices:
        copy.wait_recv()
    wide = [
        remote(every.at[block], every.at[block], wide_send.at[off - 1], wide_recv.at[off - 1],
               {"dp": (block + off) % dp_count})
        for off in range(1, dp_count)
    ]
    for copy in wide:
        copy.start()
    for copy in wide:
        copy.wait_recv()

    recs = packed.shape[2]
    total = jnp.zeros((4 * recs, dp_count * 4 * recs), jnp.float32)
    for plane in range(depth):
        lhs = every[block, :, plane].astype(jnp.float32).reshape(4 * recs, LANES).astype(jnp.bfloat16)
        rhs = every[:, :, plane].astype(jnp.float32).reshape(dp_count * 4 * recs, LANES).astype(jnp.bfloat16)
        total += lax.dot_general(lhs, rhs, (((1,), (1,)), ((), ())), preferred_element_type=jnp.float32)
    for j in range(4):
        sums[j] = total[j * recs:(j + 1) * recs]
    rows = []
    for off in range(1, 4):
        peer = (me + off) % 4
        rows.append(
            remote(sums.at[peer], got.at[off - 1], row_send.at[off - 1], row_recv.at[off - 1], {"tensor": peer})
        )
    for copy in rows:
        copy.start()
    result = sums[me]
    for off in range(3):
        rows[off].wait_recv()
        result = result + got[off]
    out_ref[...] = result
    for copy in first + second + over + slices + wide + rows:
        copy.wait_send()


def share(lefts, right_part, dp_count):
    pairs, _, steps_out = lefts[0].shape
    recs = 2 * pairs
    depth = LANES // 16
    vmem = pl.BlockSpec(memory_space=pltpu.VMEM)
    dma = pltpu.SemaphoreType.DMA
    return pl.pallas_call(
        functools.partial(share_kernel, dp_count),
        out_shape=jax.ShapeDtypeStruct((recs, dp_count * 4 * recs), jnp.float32),
        in_specs=[vmem] * 5,
        out_specs=vmem,
        scratch_shapes=[
            pltpu.VMEM((pairs, steps_out, LANES), jnp.float32),
            pltpu.VMEM((pairs, steps_out, LANES), jnp.float32),
            pltpu.VMEM((pairs, steps_out, LANES), jnp.bfloat16),
            pltpu.VMEM((pairs, steps_out, LANES), jnp.bfloat16),
            pltpu.VMEM((4 * depth, recs, LANES), jnp.float32),
            pltpu.VMEM((4, depth, recs, LANES), jnp.bfloat16),
            pltpu.VMEM((dp_count, 4, depth, recs, LANES), jnp.bfloat16),
            pltpu.VMEM((4, recs, dp_count * 4 * recs), jnp.float32),
            pltpu.VMEM((3, recs, dp_count * 4 * recs), jnp.float32),
            dma((2 * pairs,)), dma((2 * pairs,)), dma((pairs,)), dma((pairs,)),
            dma((3,)), dma((3,)), dma((dp_count - 1,)), dma((dp_count - 1,)), dma((3,)), dma((3,)),
        ],
        compiler_params=pltpu.CompilerParams(
            collective_id=0, has_side_effects=True, vmem_limit_bytes=40 * 1024 * 1024
        ),
    )(*lefts, right_part)


def left_part_of(lengths, cotangent, proj_a):
    steps_out = cotangent.shape[2]
    outpos = 2 * jnp.arange(steps_out, dtype=jnp.int32)
    tkeep = outpos[None, :] < lengths[:, None]
    masked = jnp.where(tkeep[:, None, :], cotangent, jnp.zeros((), cotangent.dtype))
    return jnp.einsum("nct,ca->nat", masked, proj_a, preferred_element_type=jnp.float32)


def local(token_ids, lengths, table, cotangent, proj_a, proj_b):
    recipes_here, seqlen = token_ids.shape
    chans, width = proj_a.shape
    vocab = table.shape[1]
    steps_out = seqlen // 2
    total_feats = width * width
    left_part = left_part_of(lengths, cotangent, proj_a)

    pos = jnp.arange(seqlen, dtype=jnp.int32)
    ids = jnp.where(pos[None, :] < lengths[:, None], token_ids, vocab)
    live = (lengths + 1) // 2
    weights = jnp.transpose(proj_b, (1, 2, 0))
    if lax.axis_size("tensor") == 4:
        mine = recipes_here // 4
        me = lax.axis_index("tensor")
        pieces = left_part.reshape(4, mine // 2, 2 * width, steps_out)
        partners = [[j + 1 - 2 * (j % 2) for j in range(4)], [(j + 2) % 4 for j in range(4)]]
        partners.append([(j + 2) % 4 for j in partners[0]])
        offsets = [1 - 2 * (me % 2), 2, 3 - 2 * (me % 2)]
        own = lax.dynamic_index_in_dim(pieces, me, 0, keepdims=False)
        gifts = [lax.dynamic_index_in_dim(pieces, (me + off) % 4, 0, keepdims=False) for off in offsets]
        weights, *gifts = lax.optimization_barrier((weights, *gifts))
        lefts = [own] + [
            lax.ppermute(gift, "tensor", list(enumerate(to))) for gift, to in zip(gifts, partners)
        ]
        right_part = right_pairs(ids, live, table, weights, steps_out)
        return share(lefts, right_part, lax.axis_size("dp")) * (1.0 / total_feats)
    left_own = lax.psum_scatter(left_part, "tensor", scatter_dimension=0, tiled=True)
    right_part = right_pairs(ids, live, table, weights, steps_out)
    right_own = lax.psum_scatter(right_part, "tensor", scatter_dimension=0, tiled=True)
    mine = right_own.shape[0] * 2
    left_two = left_own.reshape(mine // 2, 2, width, steps_out)
    raw = jnp.stack(
        [
            jnp.einsum(
                "nat,ntb->nab", left_two[:, side], right_own[:, :, side * width:(side + 1) * width],
                precision=lax.Precision.HIGHEST,
            )
            for side in range(2)
        ],
        axis=1,
    ).reshape(mine, total_feats)
    scale = lax.rsqrt(jnp.mean(raw * raw, axis=1) + 1e-06)
    unit = (raw * scale[:, None]).astype(jnp.bfloat16)
    every = lax.all_gather(unit, ("dp", "tensor"), axis=0, tiled=True)
    terms = lax.dot_general(
        unit, every, (((1,), (1,)), ((), ())), preferred_element_type=jnp.float32
    )
    return terms * (1.0 / total_feats)


def solution(mesh):
    placed = (
        P("dp", None),
        P("dp"),
        P("tensor", None),
        P("dp", "tensor", None),
        P("tensor", None),
        P("tensor", None, None),
    )
    return jax.shard_map(
        local, mesh=mesh, in_specs=placed, out_specs=P(("dp", "tensor"), None), check_vma=False
    )
```

```python
import functools

import jax
import jax.numpy as jnp
from jax import lax
from jax.experimental import pallas as pl
from jax.experimental.pallas import tpu as pltpu
from jax.sharding import PartitionSpec as P

LANES = 128
UNROLL = 16
PAD = 16
CHUNK = 640


def right_kernel(vocab, vblocks, group, steps_out, ids_ref, live_ref, table_ref, w_ref, out_ref, rows, near, far, wts):
    step = pl.program_id(0)
    vblk = table_ref.shape[1]

    @pl.when(step == 0)
    def _():
        tap = [w_ref[k] for k in range(5)]
        wts[...] = jnp.concatenate([tap[2], tap[0], tap[3], tap[1], jnp.zeros_like(tap[4]), tap[4]], axis=0)

    @pl.when(step < vblocks)
    def _():
        def project(i, _):
            at = pl.multiple_of(i * CHUNK, LANES)
            base = pl.multiple_of(step * vblk + at, LANES)
            part = lax.dot_general(
                table_ref[:, pl.ds(at, CHUNK)], wts[...], (((0,), (1,)), ((), ())),
                preferred_element_type=jnp.float32,
            )
            for col in range(3):
                rows[col, pl.ds(base, CHUNK), :] = part[:, col * LANES:(col + 1) * LANES]
            return 0

        lax.fori_loop(0, vblk // CHUNK, project, 0, unroll=True)

    @pl.when(step == vblocks)
    def _():
        for col in range(3):
            rows[col, pl.ds(vocab, PAD), :] = jnp.zeros((PAD, LANES), jnp.float32)
        for side in range(2):
            near[side, pl.ds(0, PAD), :] = jnp.zeros((PAD, LANES), jnp.float32)
            far[side, pl.ds(PAD + steps_out, PAD), :] = jnp.zeros((PAD, LANES), jnp.float32)

    @pl.when(step >= vblocks)
    def _():
        lane = lax.broadcasted_iota(jnp.int32, (steps_out, LANES), 1)
        for pair in range(group // 2):
            for side in range(2):
                rec = (step - vblocks) * group + pair * 2 + side
                live = live_ref[rec]
                tiles = (live + (UNROLL - 1)) // UNROLL

                def clear(i, _):
                    at = pl.ds(pl.multiple_of(PAD + i * UNROLL, UNROLL), UNROLL)
                    near[side, at, :] = jnp.zeros((UNROLL, LANES), jnp.float32)
                    far[side, at, :] = jnp.zeros((UNROLL, LANES), jnp.float32)
                    return 0

                lax.fori_loop(tiles, steps_out // UNROLL, clear, 0)

                def fetch(i, _):
                    start = rec * (2 * steps_out) + i * (2 * UNROLL)
                    for u in range(UNROLL):
                        even = ids_ref[start + 2 * u]
                        odd = ids_ref[start + 2 * u + 1]
                        at = pl.ds(PAD + i * UNROLL + u, 1)
                        near[side, at, :] = rows[0, pl.ds(even, 1), :] + rows[1, pl.ds(odd, 1), :]
                        far[side, at, :] = rows[2, pl.ds(even, 1), :]
                    return 0

                lax.fori_loop(0, tiles, fetch, 0)
            own0 = near[0, pl.ds(PAD, steps_out), :]
            own1 = near[1, pl.ds(PAD, steps_out), :]
            edge0 = near[0, pl.ds(PAD - 1, steps_out), :] + far[0, pl.ds(PAD + 1, steps_out), :]
            edge1 = near[1, pl.ds(PAD - 1, steps_out), :] + far[1, pl.ds(PAD + 1, steps_out), :]
            first = own0 + pltpu.roll(edge0, LANES // 2, 1)
            second = pltpu.roll(own1, LANES // 2, 1) + edge1
            out_ref[pair] = jnp.where(lane < LANES // 2, first, second)


def right_pairs(ids, live, table, weights, steps_out):
    vocab = table.shape[1]
    chans = table.shape[0]
    recipes = live.shape[0]
    vblk = 5 * CHUNK
    vblocks = vocab // vblk
    group = 4
    return pl.pallas_call(
        functools.partial(right_kernel, vocab, vblocks, group, steps_out),
        grid_spec=pltpu.PrefetchScalarGridSpec(
            num_scalar_prefetch=2,
            grid=(vblocks + recipes // group,),
            in_specs=[
                pl.BlockSpec((chans, vblk), lambda s, *_: (0, jnp.minimum(s, vblocks - 1))),
                pl.BlockSpec(weights.shape, lambda s, *_: (0, 0, 0)),
            ],
            out_specs=pl.BlockSpec(
                (group // 2, steps_out, LANES), lambda s, *_: (jnp.maximum(s - vblocks, 0), 0, 0)
            ),
            scratch_shapes=[
                pltpu.VMEM((3, vocab + PAD, LANES), jnp.float32),
                pltpu.VMEM((2, steps_out + 2 * PAD, LANES), jnp.float32),
                pltpu.VMEM((2, steps_out + 2 * PAD, LANES), jnp.float32),
                pltpu.VMEM((3 * LANES, chans), jnp.bfloat16),
            ],
        ),
        out_shape=jax.ShapeDtypeStruct((recipes // 2, steps_out, LANES), jnp.float32),
        compiler_params=pltpu.CompilerParams(vmem_limit_bytes=60 * 1024 * 1024),
        cost_estimate=pl.CostEstimate(
            flops=2 * vocab * chans * 3 * LANES, bytes_accessed=200 * 1024 * 1024, transcendentals=0
        ),
    )(ids, live, table, weights)


def share_kernel(dp_count, left_ref, left_b, left_c, left_d, part_ref, out_ref, core_in, core_own, cross_out, cross_in,
                 planes, packed, every, sums, got, core_send, core_recv, cross_send, cross_recv,
                 slice_send, slice_recv, wide_send, wide_recv, row_send, row_recv,
                 held, keep_sem, pass_send, pass_recv):
    me = lax.axis_index("tensor")
    block = lax.axis_index("dp")
    sib = me + 1 - 2 * (me % 2)
    across = (me + 2) % 4
    diag = (sib + 2) % 4
    pairs = left_ref.shape[0]
    half = LANES // 2
    feats = half * half
    mesh_ids = pl.DeviceIdType.MESH

    barrier = pltpu.get_barrier_semaphore()
    for off in range(1, 4):
        pl.semaphore_signal(barrier, inc=1, device_id={"tensor": (me + off) % 4}, device_id_type=mesh_ids)
    inner = block + 1 - 2 * (block % 2)
    hops = dp_count // 2
    for peer in [inner] + [(block + 2 * off) % dp_count for off in range(1, hops)]:
        pl.semaphore_signal(barrier, inc=1, device_id={"dp": peer}, device_id_type=mesh_ids)
    keep = [
        pltpu.make_async_copy(part_ref.at[pl.ds(owner * pairs, pairs)], held.at[k], keep_sem.at[k])
        for k, owner in enumerate((across, me))
    ]
    for copy in keep:
        copy.start()
    pl.semaphore_wait(barrier, 3 + hops)

    def remote(src, dst, send, recv, where):
        return pltpu.make_async_remote_copy(
            src_ref=src, dst_ref=dst, send_sem=send, recv_sem=recv, device_id=where, device_id_type=mesh_ids
        )

    first = [
        remote(part_ref.at[diag * pairs + i], core_in.at[i], core_send.at[i], core_recv.at[i], {"tensor": sib})
        for i in range(pairs)
    ]
    second = [
        remote(part_ref.at[sib * pairs + i], core_own.at[i], core_send.at[pairs + i], core_recv.at[pairs + i],
               {"tensor": sib})
        for i in range(pairs)
    ]
    for copy in first + second:
        copy.start()
    over = [
        remote(cross_out.at[i], cross_in.at[i], cross_send.at[i], cross_recv.at[i], {"tensor": across})
        for i in range(pairs)
    ]
    keep[0].wait()
    for i in range(pairs):
        first[i].wait_recv()
        cross_out[i] = (held[0, i] + core_in[i]).astype(jnp.bfloat16)
        over[i].start()

    lane = lax.broadcasted_iota(jnp.int32, (half // 2, LANES), 1) < half
    quarter = half // 2
    keep[1].wait()
    for i in range(pairs):
        second[i].wait_recv()
        mine = held[1, i] + core_own[i]
        over[i].wait_recv()
        right = mine + cross_in[i].astype(jnp.float32)
        raw = lax.dot_general(
            (left_ref[i] + left_b[i]) + (left_c[i] + left_d[i]), right, (((1,), (0,)), ((), ())),
            precision=lax.Precision.HIGHEST, preferred_element_type=jnp.float32,
        )
        top = jnp.where(lane, raw[:quarter], pltpu.roll(raw[quarter:half], half, 1))
        low = jnp.where(lane, pltpu.roll(raw[half:half + quarter], half, 1), raw[half + quarter:])
        for side, vals in enumerate((top, low)):
            total = jnp.sum(jnp.sum(vals * vals, axis=0, keepdims=True), axis=1, keepdims=True)
            planes[:, 2 * i + side, :] = vals * lax.rsqrt(total / feats + 1e-06)

    depth = packed.shape[1]
    for j in range(4):
        packed[j] = planes[j * depth:(j + 1) * depth].astype(jnp.bfloat16)
    every[block, me] = packed[me]
    slices = []
    for off in range(1, 4):
        peer = (me + off) % 4
        slices.append(
            remote(packed.at[peer], every.at[block, me], slice_send.at[off - 1], slice_recv.at[off - 1],
                   {"tensor": peer})
        )
    for copy in slices:
        copy.start()
    for copy in slices:
        copy.wait_recv()
    wide = [
        remote(every.at[block], every.at[block], wide_send.at[off - 1], wide_recv.at[off - 1],
               {"dp": (block + 2 * off) % dp_count})
        for off in range(1, hops)
    ]
    for copy in wide:
        copy.start()
    pass_on = []
    for off in range(hops):
        source = (block + 2 * (hops - off)) % dp_count
        pass_on.append(
            remote(every.at[source], every.at[source], pass_send.at[off], pass_recv.at[off], {"dp": inner})
        )
        if off > 0:
            wide[off - 1].wait_recv()
        pass_on[off].start()
    for copy in pass_on:
        copy.wait_recv()

    recs = packed.shape[2]
    total = jnp.zeros((4 * recs, dp_count * 4 * recs), jnp.float32)
    for plane in range(depth):
        lhs = every[block, :, plane].astype(jnp.float32).reshape(4 * recs, LANES).astype(jnp.bfloat16)
        rhs = every[:, :, plane].astype(jnp.float32).reshape(dp_count * 4 * recs, LANES).astype(jnp.bfloat16)
        total += lax.dot_general(lhs, rhs, (((1,), (1,)), ((), ())), preferred_element_type=jnp.float32)
    for j in range(4):
        sums[j] = total[j * recs:(j + 1) * recs]
    rows = []
    for off in range(1, 4):
        peer = (me + off) % 4
        rows.append(
            remote(sums.at[peer], got.at[off - 1], row_send.at[off - 1], row_recv.at[off - 1], {"tensor": peer})
        )
    for copy in rows:
        copy.start()
    result = sums[me]
    for off in range(3):
        rows[off].wait_recv()
        result = result + got[off]
    out_ref[...] = result
    for copy in first + second + over + slices + wide + pass_on + rows:
        copy.wait_send()


def share(lefts, right_part, dp_count):
    pairs, _, steps_out = lefts[0].shape
    recs = 2 * pairs
    depth = LANES // 16
    vmem = pl.BlockSpec(memory_space=pltpu.VMEM)
    dma = pltpu.SemaphoreType.DMA
    return pl.pallas_call(
        functools.partial(share_kernel, dp_count),
        out_shape=jax.ShapeDtypeStruct((recs, dp_count * 4 * recs), jnp.float32),
        in_specs=[vmem] * 4 + [pl.BlockSpec(memory_space=pl.ANY)],
        out_specs=vmem,
        scratch_shapes=[
            pltpu.VMEM((pairs, steps_out, LANES), jnp.float32),
            pltpu.VMEM((pairs, steps_out, LANES), jnp.float32),
            pltpu.VMEM((pairs, steps_out, LANES), jnp.bfloat16),
            pltpu.VMEM((pairs, steps_out, LANES), jnp.bfloat16),
            pltpu.VMEM((4 * depth, recs, LANES), jnp.float32),
            pltpu.VMEM((4, depth, recs, LANES), jnp.bfloat16),
            pltpu.VMEM((dp_count, 4, depth, recs, LANES), jnp.bfloat16),
            pltpu.VMEM((4, recs, dp_count * 4 * recs), jnp.float32),
            pltpu.VMEM((3, recs, dp_count * 4 * recs), jnp.float32),
            dma((2 * pairs,)), dma((2 * pairs,)), dma((pairs,)), dma((pairs,)),
            dma((3,)), dma((3,)), dma((dp_count // 2 - 1,)), dma((dp_count // 2 - 1,)), dma((3,)), dma((3,)),
            pltpu.VMEM((2, pairs, steps_out, LANES), jnp.float32),
            dma((2,)), dma((dp_count // 2,)), dma((dp_count // 2,)),
        ],
        compiler_params=pltpu.CompilerParams(
            collective_id=0, has_side_effects=True, vmem_limit_bytes=40 * 1024 * 1024
        ),
    )(*lefts, right_part)


def left_part_of(lengths, cotangent, proj_a):
    steps_out = cotangent.shape[2]
    outpos = 2 * jnp.arange(steps_out, dtype=jnp.int32)
    tkeep = outpos[None, :] < lengths[:, None]
    masked = jnp.where(tkeep[:, None, :], cotangent, jnp.zeros((), cotangent.dtype))
    return jnp.einsum("nct,ca->nat", masked, proj_a, preferred_element_type=jnp.float32)


def local(token_ids, lengths, table, cotangent, proj_a, proj_b):
    recipes_here, seqlen = token_ids.shape
    chans, width = proj_a.shape
    vocab = table.shape[1]
    steps_out = seqlen // 2
    total_feats = width * width
    left_part = left_part_of(lengths, cotangent, proj_a)

    pos = jnp.arange(seqlen, dtype=jnp.int32)
    ids = jnp.where(pos[None, :] < lengths[:, None], token_ids, vocab).reshape(-1)
    live = (lengths + 1) // 2
    weights = jnp.transpose(proj_b, (1, 2, 0))
    if lax.axis_size("tensor") == 4:
        mine = recipes_here // 4
        me = lax.axis_index("tensor")
        pieces = left_part.reshape(4, mine // 2, 2 * width, steps_out)
        partners = [[j + 1 - 2 * (j % 2) for j in range(4)], [(j + 2) % 4 for j in range(4)]]
        partners.append([(j + 2) % 4 for j in partners[0]])
        offsets = [1 - 2 * (me % 2), 2, 3 - 2 * (me % 2)]
        own = lax.dynamic_index_in_dim(pieces, me, 0, keepdims=False)
        gifts = [lax.dynamic_index_in_dim(pieces, (me + off) % 4, 0, keepdims=False) for off in offsets]
        weights, *gifts = lax.optimization_barrier((weights, *gifts))
        lefts = [own] + [
            lax.ppermute(gift, "tensor", list(enumerate(to))) for gift, to in zip(gifts, partners)
        ]
        right_part = right_pairs(ids, live, table, weights, steps_out)
        return share(lefts, right_part, lax.axis_size("dp")) * (1.0 / total_feats)
    left_own = lax.psum_scatter(left_part, "tensor", scatter_dimension=0, tiled=True)
    right_part = right_pairs(ids, live, table, weights, steps_out)
    right_own = lax.psum_scatter(right_part, "tensor", scatter_dimension=0, tiled=True)
    mine = right_own.shape[0] * 2
    left_two = left_own.reshape(mine // 2, 2, width, steps_out)
    raw = jnp.stack(
        [
            jnp.einsum(
                "nat,ntb->nab", left_two[:, side], right_own[:, :, side * width:(side + 1) * width],
                precision=lax.Precision.HIGHEST,
            )
            for side in range(2)
        ],
        axis=1,
    ).reshape(mine, total_feats)
    scale = lax.rsqrt(jnp.mean(raw * raw, axis=1) + 1e-06)
    unit = (raw * scale[:, None]).astype(jnp.bfloat16)
    every = lax.all_gather(unit, ("dp", "tensor"), axis=0, tiled=True)
    terms = lax.dot_general(
        unit, every, (((1,), (1,)), ((), ())), preferred_element_type=jnp.float32
    )
    return terms * (1.0 / total_feats)


def solution(mesh):
    placed = (
        P("dp", None),
        P("dp"),
        P("tensor", None),
        P("dp", "tensor", None),
        P("tensor", None),
        P("tensor", None, None),
    )
    return jax.shard_map(
        local, mesh=mesh, in_specs=placed, out_specs=P(("dp", "tensor"), None), check_vma=False
    )
```

```python
import functools

import jax
import jax.numpy as jnp
from jax import lax
from jax.experimental import pallas as pl
from jax.experimental.pallas import tpu as pltpu
from jax.sharding import PartitionSpec as P

LANES = 128
UNROLL = 32
PAD = 32
CHUNK = 640


def right_kernel(vocab, vblocks, group, steps_out, ids_ref, live_ref, table_ref, w_ref, out_ref, rows, near, far, wts):
    step = pl.program_id(0)
    vblk = table_ref.shape[1]

    @pl.when(step == 0)
    def _():
        tap = [w_ref[k] for k in range(5)]
        wts[...] = jnp.concatenate([tap[2], tap[0], tap[3], tap[1], jnp.zeros_like(tap[4]), tap[4]], axis=0)

    @pl.when(step < vblocks)
    def _():
        def project(i, _):
            at = pl.multiple_of(i * CHUNK, LANES)
            base = pl.multiple_of(step * vblk + at, LANES)
            part = lax.dot_general(
                table_ref[:, pl.ds(at, CHUNK)], wts[...], (((0,), (1,)), ((), ())),
                preferred_element_type=jnp.float32,
            )
            for col in range(3):
                rows[col, pl.ds(base, CHUNK), :] = part[:, col * LANES:(col + 1) * LANES]
            return 0

        lax.fori_loop(0, vblk // CHUNK, project, 0, unroll=True)

    @pl.when(step == vblocks)
    def _():
        for col in range(3):
            rows[col, pl.ds(vocab, PAD), :] = jnp.zeros((PAD, LANES), jnp.float32)
        for side in range(2):
            near[side, pl.ds(0, PAD), :] = jnp.zeros((PAD, LANES), jnp.float32)
            far[side, pl.ds(PAD + steps_out, PAD), :] = jnp.zeros((PAD, LANES), jnp.float32)

    @pl.when(step >= vblocks)
    def _():
        lane = lax.broadcasted_iota(jnp.int32, (steps_out, LANES), 1)
        for pair in range(group // 2):
            for side in range(2):
                rec = (step - vblocks) * group + pair * 2 + side
                live = live_ref[rec]
                tiles = (live + (UNROLL - 1)) // UNROLL

                def clear(i, _):
                    at = pl.ds(pl.multiple_of(PAD + i * UNROLL, UNROLL), UNROLL)
                    near[side, at, :] = jnp.zeros((UNROLL, LANES), jnp.float32)
                    far[side, at, :] = jnp.zeros((UNROLL, LANES), jnp.float32)
                    return 0

                lax.fori_loop(tiles, steps_out // UNROLL, clear, 0)

                def fetch(i, _):
                    start = rec * (2 * steps_out) + i * (2 * UNROLL)
                    for u in range(UNROLL):
                        even = ids_ref[start + 2 * u]
                        odd = ids_ref[start + 2 * u + 1]
                        at = pl.ds(PAD + i * UNROLL + u, 1)
                        near[side, at, :] = rows[0, pl.ds(even, 1), :] + rows[1, pl.ds(odd, 1), :]
                        far[side, at, :] = rows[2, pl.ds(even, 1), :]
                    return 0

                lax.fori_loop(0, tiles, fetch, 0)
            own0 = near[0, pl.ds(PAD, steps_out), :]
            own1 = near[1, pl.ds(PAD, steps_out), :]
            edge0 = near[0, pl.ds(PAD - 1, steps_out), :] + far[0, pl.ds(PAD + 1, steps_out), :]
            edge1 = near[1, pl.ds(PAD - 1, steps_out), :] + far[1, pl.ds(PAD + 1, steps_out), :]
            first = own0 + pltpu.roll(edge0, LANES // 2, 1)
            second = pltpu.roll(own1, LANES // 2, 1) + edge1
            out_ref[pair] = jnp.where(lane < LANES // 2, first, second)


def right_pairs(ids, live, table, weights, steps_out):
    vocab = table.shape[1]
    chans = table.shape[0]
    recipes = live.shape[0]
    vblk = 5 * CHUNK
    vblocks = vocab // vblk
    group = 8
    return pl.pallas_call(
        functools.partial(right_kernel, vocab, vblocks, group, steps_out),
        grid_spec=pltpu.PrefetchScalarGridSpec(
            num_scalar_prefetch=2,
            grid=(vblocks + recipes // group,),
            in_specs=[
                pl.BlockSpec((chans, vblk), lambda s, *_: (0, jnp.minimum(s, vblocks - 1))),
                pl.BlockSpec(weights.shape, lambda s, *_: (0, 0, 0)),
            ],
            out_specs=pl.BlockSpec(
                (group // 2, steps_out, LANES), lambda s, *_: (jnp.maximum(s - vblocks, 0), 0, 0)
            ),
            scratch_shapes=[
                pltpu.VMEM((3, vocab + PAD, LANES), jnp.float32),
                pltpu.VMEM((2, steps_out + 2 * PAD, LANES), jnp.float32),
                pltpu.VMEM((2, steps_out + 2 * PAD, LANES), jnp.float32),
                pltpu.VMEM((3 * LANES, chans), jnp.bfloat16),
            ],
        ),
        out_shape=jax.ShapeDtypeStruct((recipes // 2, steps_out, LANES), jnp.float32),
        compiler_params=pltpu.CompilerParams(vmem_limit_bytes=60 * 1024 * 1024),
        cost_estimate=pl.CostEstimate(
            flops=2 * vocab * chans * 3 * LANES, bytes_accessed=200 * 1024 * 1024, transcendentals=0
        ),
    )(ids, live, table, weights)


def share_kernel(dp_count, left_ref, left_b, left_c, left_d, part_ref, out_ref, core_in, core_own, cross_out, cross_in,
                 planes, packed, every, sums, got, core_send, core_recv, cross_send, cross_recv,
                 slice_send, slice_recv, wide_send, wide_recv, row_send, row_recv,
                 held, keep_sem, pass_send, pass_recv):
    me = lax.axis_index("tensor")
    block = lax.axis_index("dp")
    sib = me + 1 - 2 * (me % 2)
    across = (me + 2) % 4
    diag = (sib + 2) % 4
    pairs = left_ref.shape[0]
    half = LANES // 2
    feats = half * half
    mesh_ids = pl.DeviceIdType.MESH

    barrier = pltpu.get_barrier_semaphore()
    for off in range(1, 4):
        pl.semaphore_signal(barrier, inc=1, device_id={"tensor": (me + off) % 4}, device_id_type=mesh_ids)
    inner = block + 1 - 2 * (block % 2)
    hops = dp_count // 2
    for peer in [inner] + [(block + 2 * off) % dp_count for off in range(1, hops)]:
        pl.semaphore_signal(barrier, inc=1, device_id={"dp": peer}, device_id_type=mesh_ids)
    keep = [
        pltpu.make_async_copy(part_ref.at[pl.ds(owner * pairs, pairs)], held.at[k], keep_sem.at[k])
        for k, owner in enumerate((across, me))
    ]
    for copy in keep:
        copy.start()
    pl.semaphore_wait(barrier, 3 + hops)

    def remote(src, dst, send, recv, where):
        return pltpu.make_async_remote_copy(
            src_ref=src, dst_ref=dst, send_sem=send, recv_sem=recv, device_id=where, device_id_type=mesh_ids
        )

    first = [
        remote(part_ref.at[diag * pairs + i], core_in.at[i], core_send.at[i], core_recv.at[i], {"tensor": sib})
        for i in range(pairs)
    ]
    second = [
        remote(part_ref.at[sib * pairs + i], core_own.at[i], core_send.at[pairs + i], core_recv.at[pairs + i],
               {"tensor": sib})
        for i in range(pairs)
    ]
    for copy in first + second:
        copy.start()
    over = [
        remote(cross_out.at[i], cross_in.at[i], cross_send.at[i], cross_recv.at[i], {"tensor": across})
        for i in range(pairs)
    ]
    keep[0].wait()
    for i in range(pairs):
        first[i].wait_recv()
        cross_out[i] = (held[0, i] + core_in[i]).astype(jnp.bfloat16)
        over[i].start()

    lane = lax.broadcasted_iota(jnp.int32, (half // 2, LANES), 1) < half
    quarter = half // 2
    keep[1].wait()
    for i in range(pairs):
        second[i].wait_recv()
        mine = held[1, i] + core_own[i]
        over[i].wait_recv()
        right = mine + cross_in[i].astype(jnp.float32)
        raw = lax.dot_general(
            (left_ref[i] + left_b[i]) + (left_c[i] + left_d[i]), right, (((1,), (0,)), ((), ())),
            precision=lax.Precision.HIGHEST, preferred_element_type=jnp.float32,
        )
        top = jnp.where(lane, raw[:quarter], pltpu.roll(raw[quarter:half], half, 1))
        low = jnp.where(lane, pltpu.roll(raw[half:half + quarter], half, 1), raw[half + quarter:])
        for side, vals in enumerate((top, low)):
            total = jnp.sum(jnp.sum(vals * vals, axis=0, keepdims=True), axis=1, keepdims=True)
            planes[:, 2 * i + side, :] = vals * lax.rsqrt(total / feats + 1e-06)

    depth = packed.shape[1]
    for j in range(4):
        packed[j] = planes[j * depth:(j + 1) * depth].astype(jnp.bfloat16)
    every[block, me] = packed[me]
    slices = []
    for off in range(1, 4):
        peer = (me + off) % 4
        slices.append(
            remote(packed.at[peer], every.at[block, me], slice_send.at[off - 1], slice_recv.at[off - 1],
                   {"tensor": peer})
        )
    for copy in slices:
        copy.start()
    for copy in slices:
        copy.wait_recv()
    wide = [
        remote(every.at[block], every.at[block], wide_send.at[off - 1], wide_recv.at[off - 1],
               {"dp": (block + 2 * off) % dp_count})
        for off in range(1, hops)
    ]
    for copy in wide:
        copy.start()
    pass_on = []
    for off in range(hops):
        source = (block + 2 * (hops - off)) % dp_count
        pass_on.append(
            remote(every.at[source], every.at[source], pass_send.at[off], pass_recv.at[off], {"dp": inner})
        )
        if off > 0:
            wide[off - 1].wait_recv()
        pass_on[off].start()
    for copy in pass_on:
        copy.wait_recv()

    recs = packed.shape[2]
    total = jnp.zeros((4 * recs, dp_count * 4 * recs), jnp.float32)
    for plane in range(depth):
        lhs = every[block, :, plane].astype(jnp.float32).reshape(4 * recs, LANES).astype(jnp.bfloat16)
        rhs = every[:, :, plane].astype(jnp.float32).reshape(dp_count * 4 * recs, LANES).astype(jnp.bfloat16)
        total += lax.dot_general(lhs, rhs, (((1,), (1,)), ((), ())), preferred_element_type=jnp.float32)
    for j in range(4):
        sums[j] = total[j * recs:(j + 1) * recs]
    rows = []
    for off in range(1, 4):
        peer = (me + off) % 4
        rows.append(
            remote(sums.at[peer], got.at[off - 1], row_send.at[off - 1], row_recv.at[off - 1], {"tensor": peer})
        )
    for copy in rows:
        copy.start()
    result = sums[me]
    for off in range(3):
        rows[off].wait_recv()
        result = result + got[off]
    out_ref[...] = result
    for copy in first + second + over + slices + wide + pass_on + rows:
        copy.wait_send()


def share(lefts, right_part, dp_count):
    pairs, _, steps_out = lefts[0].shape
    recs = 2 * pairs
    depth = LANES // 16
    vmem = pl.BlockSpec(memory_space=pltpu.VMEM)
    dma = pltpu.SemaphoreType.DMA
    return pl.pallas_call(
        functools.partial(share_kernel, dp_count),
        out_shape=jax.ShapeDtypeStruct((recs, dp_count * 4 * recs), jnp.float32),
        in_specs=[vmem] * 4 + [pl.BlockSpec(memory_space=pl.ANY)],
        out_specs=vmem,
        scratch_shapes=[
            pltpu.VMEM((pairs, steps_out, LANES), jnp.float32),
            pltpu.VMEM((pairs, steps_out, LANES), jnp.float32),
            pltpu.VMEM((pairs, steps_out, LANES), jnp.bfloat16),
            pltpu.VMEM((pairs, steps_out, LANES), jnp.bfloat16),
            pltpu.VMEM((4 * depth, recs, LANES), jnp.float32),
            pltpu.VMEM((4, depth, recs, LANES), jnp.bfloat16),
            pltpu.VMEM((dp_count, 4, depth, recs, LANES), jnp.bfloat16),
            pltpu.VMEM((4, recs, dp_count * 4 * recs), jnp.float32),
            pltpu.VMEM((3, recs, dp_count * 4 * recs), jnp.float32),
            dma((2 * pairs,)), dma((2 * pairs,)), dma((pairs,)), dma((pairs,)),
            dma((3,)), dma((3,)), dma((dp_count // 2 - 1,)), dma((dp_count // 2 - 1,)), dma((3,)), dma((3,)),
            pltpu.VMEM((2, pairs, steps_out, LANES), jnp.float32),
            dma((2,)), dma((dp_count // 2,)), dma((dp_count // 2,)),
        ],
        compiler_params=pltpu.CompilerParams(
            collective_id=0, has_side_effects=True, vmem_limit_bytes=40 * 1024 * 1024
        ),
    )(*lefts, right_part)


def left_part_of(lengths, cotangent, proj_a):
    steps_out = cotangent.shape[2]
    outpos = 2 * jnp.arange(steps_out, dtype=jnp.int32)
    tkeep = outpos[None, :] < lengths[:, None]
    masked = jnp.where(tkeep[:, None, :], cotangent, jnp.zeros((), cotangent.dtype))
    return jnp.einsum("nct,ca->nat", masked, proj_a, preferred_element_type=jnp.float32)


def local(token_ids, lengths, table, cotangent, proj_a, proj_b):
    recipes_here, seqlen = token_ids.shape
    chans, width = proj_a.shape
    vocab = table.shape[1]
    steps_out = seqlen // 2
    total_feats = width * width
    left_part = left_part_of(lengths, cotangent, proj_a)

    pos = jnp.arange(seqlen, dtype=jnp.int32)
    ids = jnp.where(pos[None, :] < lengths[:, None], token_ids, vocab).reshape(-1)
    live = (lengths + 1) // 2
    weights = jnp.transpose(proj_b, (1, 2, 0))
    if lax.axis_size("tensor") == 4:
        mine = recipes_here // 4
        me = lax.axis_index("tensor")
        pieces = left_part.reshape(4, mine // 2, 2 * width, steps_out)
        partners = [[j + 1 - 2 * (j % 2) for j in range(4)], [(j + 2) % 4 for j in range(4)]]
        partners.append([(j + 2) % 4 for j in partners[0]])
        offsets = [1 - 2 * (me % 2), 2, 3 - 2 * (me % 2)]
        own = lax.dynamic_index_in_dim(pieces, me, 0, keepdims=False)
        gifts = [lax.dynamic_index_in_dim(pieces, (me + off) % 4, 0, keepdims=False) for off in offsets]
        weights, *gifts = lax.optimization_barrier((weights, *gifts))
        lefts = [own] + [
            lax.ppermute(gift, "tensor", list(enumerate(to))) for gift, to in zip(gifts, partners)
        ]
        right_part = right_pairs(ids, live, table, weights, steps_out)
        return share(lefts, right_part, lax.axis_size("dp")) * (1.0 / total_feats)
    left_own = lax.psum_scatter(left_part, "tensor", scatter_dimension=0, tiled=True)
    right_part = right_pairs(ids, live, table, weights, steps_out)
    right_own = lax.psum_scatter(right_part, "tensor", scatter_dimension=0, tiled=True)
    mine = right_own.shape[0] * 2
    left_two = left_own.reshape(mine // 2, 2, width, steps_out)
    raw = jnp.stack(
        [
            jnp.einsum(
                "nat,ntb->nab", left_two[:, side], right_own[:, :, side * width:(side + 1) * width],
                precision=lax.Precision.HIGHEST,
            )
            for side in range(2)
        ],
        axis=1,
    ).reshape(mine, total_feats)
    scale = lax.rsqrt(jnp.mean(raw * raw, axis=1) + 1e-06)
    unit = (raw * scale[:, None]).astype(jnp.bfloat16)
    every = lax.all_gather(unit, ("dp", "tensor"), axis=0, tiled=True)
    terms = lax.dot_general(
        unit, every, (((1,), (1,)), ((), ())), preferred_element_type=jnp.float32
    )
    return terms * (1.0 / total_feats)


def solution(mesh):
    placed = (
        P("dp", None),
        P("dp"),
        P("tensor", None),
        P("dp", "tensor", None),
        P("tensor", None),
        P("tensor", None, None),
    )
    return jax.shard_map(
        local, mesh=mesh, in_specs=placed, out_specs=P(("dp", "tensor"), None), check_vma=False
    )
```
